32 devices in a mesh: row: 4 (over z), col: 8 (over y, x, core).
Axes of the slice: x: 2, y: 2, z: 4, core: 2. Of those that a mesh axis runs over, the one named last changes fastest.
Arguments:
- coords: float32 [3, 4096], P(None, ('row', 'col')), may hold values from -1 to 1
- residual_in: float32 [4096, 512], P(('row', 'col')), may hold values from -6 to 6
- link_mask: int32 [32, 2], P(('row', 'col')), may hold values 0 or 1
- compress: float32 [4096, 256], P(('row', 'col')), may hold values from -0.5 to 0.5
- expand: float32 [4096, 256], P(('row', 'col')), may hold values from -0.375 to 0.375
- level_gain: float32 [32, 1280], P(('row', 'col')), may hold values from 0.5 to 1.5
- level_couple: float32 [8192, 1280], P(('row', 'col')), may hold values from -0.1875 to 0.1875
- partner_perm: int32 [32, 5, 256], P(('row', 'col')), may hold values from 0 to 255, each once within a row
Outputs:
- new_residual: float32 [4096, 512], P(('row', 'col'))
- res_norms: float32 [512], replicated
The draws below stay inside these ranges and needn't reach their ends.
Inputs may be any that keep to these rules, and one draw needn't show every extreme that they name: `partner_perm`: each row of 256 entries names every number once.
All inputs are finite; a program needn't handle non-finite values. No bound on the sum of `link_mask` on one device may be relied on, other than what follows from the above.
Results may differ from the reference program's by a relative error of at most 0.0003.
Values sent between devices are 32-bit elements; how exact they have to be, the bound alone decides.
A program may use at most 64 MiB of HBM per device.

```python
import jax
import jax.numpy as jnp
import numpy as np
from jax import lax

P_DEV = 128
RHS = 512
RANK = 256
ROW_LEVELS = 2
COL_LEVELS = 3
LEVELS = 5
GROUPS = 32
POINTS = 4096
N_ROW = 4
N_COL = 8


def draw_residual_in(key, part):
    folded = jax.random.fold_in(key, 17)
    key_rotation = jax.random.fold_in(folded, 1)
    key_bulk = jax.random.fold_in(folded, 2)
    rotation = jnp.linalg.qr(jax.random.normal(key_rotation, (RHS, RHS), jnp.float32))[0]
    spread_vals = 10.0 ** jnp.linspace(0.0, -2.0, RHS, dtype=jnp.float32)
    spread_vals = spread_vals / jnp.sqrt(jnp.mean(spread_vals * spread_vals))
    mixing = jnp.dot(rotation * spread_vals[None, :], rotation.T, precision=lax.Precision.HIGHEST)
    bulk_draw = jax.random.normal(key_bulk, (POINTS, RHS), jnp.float32)
    col_scales = jnp.ones((RHS,), jnp.float32)
    mixed = jnp.dot(bulk_draw, mixing, precision=lax.Precision.HIGHEST) * col_scales[None, :]
    return jnp.clip(mixed, -6.0, 6.0)


def touch_ends(array, stream_key, smallest, largest):
    longest = array.shape.index(max(array.shape))
    spots = []
    for shift in (0, 1):
        where = [jax.random.randint(jax.random.fold_in(stream_key, axis), (), 0, length) for axis, length in enumerate(array.shape)]
        where[longest] = (where[longest] + shift) % array.shape[longest]
        spots.append(tuple(where))
    return array.at[spots[0]].set(smallest).at[spots[1]].set(largest)


def block_scale(key, dims, split, low, top_value):
    factor_of = 1.0
    for dim, blocks in split:
        heights = jax.random.uniform(jax.random.fold_in(jax.random.fold_in(key, 6), dim), (blocks,), jnp.float32, low / len(split), top_value / len(split))
        factor_of = factor_of * jnp.repeat(jnp.exp(heights), dims[dim] // blocks).reshape((-1,) + (1,) * (len(dims) - 1 - dim))
    return factor_of


def centred(rng, dims, width, reach, pieces=(), kind=jnp.bfloat16):
    gain = block_scale(rng, dims, pieces, -0.22, 0.18) if pieces else 1.0
    drawn = jax.random.normal(rng, dims, jnp.float32) * width * gain
    return jnp.minimum(jnp.maximum(drawn, -reach), reach).astype(kind)


def setup_inputs(seed: int = 0) -> dict:
    splits = jax.random.split(jax.random.key(seed), 9)
    coords = jnp.clip(jax.random.uniform(splits[0], (3, POINTS), jnp.float32, -1.0, 1.0) * block_scale(splits[0], (3, POINTS), ((1, 32),), -0.4, 0.0), -1.0, 1.0)
    residual_in = draw_residual_in(jax.random.fold_in(splits[8], 71), 0)
    link_mask = touch_ends((jax.random.randint(splits[2], (GROUPS, 2), 0, 4) < 3).astype(jnp.int32), jax.random.fold_in(splits[2], 1), 0, 1)
    compress = centred(splits[3], (POINTS, RANK), P_DEV ** -0.5, 0.5, ((0, 32),), jnp.float32)
    expand = centred(splits[4], (POINTS, RANK), RANK ** -0.5, 0.375, ((0, 32),), jnp.float32)
    level_gain = jnp.clip(1.0 + 0.1 * jax.random.normal(splits[5], (GROUPS, LEVELS * RANK), jnp.float32), 0.5, 1.5)
    level_couple = centred(splits[6], (GROUPS * RANK, LEVELS * RANK), (4 * RANK) ** -0.5, 0.1875, ((0, 32),), jnp.float32)
    partner_perm = jax.vmap(lambda own: jax.random.permutation(own, RANK))(jax.random.split(splits[7], GROUPS * LEVELS)).reshape((GROUPS, LEVELS, RANK)).astype(jnp.int32)
    return {"coords": coords, "residual_in": residual_in, "link_mask": link_mask, "compress": compress, "expand": expand, "level_gain": level_gain, "level_couple": level_couple, "partner_perm": partner_perm}


WAVENUM = 6.0
SOFTEN = 0.01

def kernel_tile(own_xyz, other_xyz):
    dist_sq = (own_xyz[0][:, None] - other_xyz[0][None, :]) ** 2
    dist_sq = dist_sq + (own_xyz[1][:, None] - other_xyz[1][None, :]) ** 2
    dist_sq = dist_sq + (own_xyz[2][:, None] - other_xyz[2][None, :]) ** 2
    return jnp.cos(WAVENUM * jnp.sqrt(dist_sq)) / jnp.sqrt(dist_sq + SOFTEN)

def matmul_hi(left, right):
    return jnp.dot(left, right, precision=lax.Precision.HIGHEST)

def chol_solve(gram_mat, cross_mat):
    factor = jnp.linalg.cholesky(gram_mat)
    middle = lax.linalg.triangular_solve(factor, cross_mat, left_side=True, lower=True)
    return lax.linalg.triangular_solve(factor, middle, left_side=True, lower=True, transpose_a=True)

def reference(coords, residual_in, link_mask, compress, expand, level_gain, level_couple, partner_perm):
    groups_all = N_ROW * N_COL
    blocks = residual_in.reshape(groups_all, P_DEV, RHS)
    xyz = coords.reshape(3, groups_all, P_DEV).transpose(1, 0, 2)
    zero_rhs = jnp.zeros((1, P_DEV, RHS), blocks.dtype)
    zero_xyz = jnp.zeros((1, 3, P_DEV), xyz.dtype)
    below_rhs = jnp.concatenate([zero_rhs, blocks[:-1]], axis=0)
    above_rhs = jnp.concatenate([blocks[1:], zero_rhs], axis=0)
    below_xyz = jnp.concatenate([zero_xyz, xyz[:-1]], axis=0)
    above_xyz = jnp.concatenate([xyz[1:], zero_xyz], axis=0)
    weights = link_mask.astype(blocks.dtype)
    near_scale = (3.0 * P_DEV) ** (-0.5)

    def near_one(items):
        own_xyz, low_xyz, high_xyz, own_rhs, low_rhs, high_rhs, mask_row = items
        total = matmul_hi(kernel_tile(own_xyz, own_xyz), own_rhs)
        total = total + mask_row[0] * matmul_hi(kernel_tile(own_xyz, low_xyz), low_rhs)
        total = total + mask_row[1] * matmul_hi(kernel_tile(own_xyz, high_xyz), high_rhs)
        return near_scale * total
    near_field = lax.map(near_one, (xyz, below_xyz, above_xyz, blocks, below_rhs, above_rhs, weights))
    comp_blocks = compress.reshape(groups_all, P_DEV, RANK)
    exp_blocks = expand.reshape(groups_all, P_DEV, RANK)
    couple_blocks = level_couple.reshape(groups_all, RANK, LEVELS * RANK)
    coeffs = jnp.einsum('dpk,dpr->dkr', comp_blocks, blocks, precision=lax.Precision.HIGHEST)
    group_ids = np.arange(groups_all)
    col_bits = N_COL.bit_length() - 1
    flips = []
    for index_row in range(ROW_LEVELS):
        flips.append(1 << N_ROW.bit_length() - 2 - index_row + col_bits)
    for index_col in range(COL_LEVELS):
        flips.append(1 << N_COL.bit_length() - 2 - index_col)
    for level_at in range(LEVELS):
        partner = coeffs[group_ids ^ flips[level_at]]
        picked = jnp.take_along_axis(partner, partner_perm[:, level_at, :, None].astype(jnp.int32), axis=1)
        gain_col = level_gain[:, level_at * RANK:(level_at + 1) * RANK][:, :, None]
        couple = couple_blocks[:, :, level_at * RANK:(level_at + 1) * RANK]
        coeffs = gain_col * coeffs + jnp.einsum('dkj,djr->dkr', couple, picked, precision=lax.Precision.HIGHEST)
    far_field = jnp.einsum('dpk,dkr->dpr', exp_blocks, coeffs, precision=lax.Precision.HIGHEST)
    image = (2.0 * blocks + near_field + far_field).reshape(POINTS, RHS)
    gram_mat = matmul_hi(image.T, image)
    cross_mat = matmul_hi(image.T, residual_in)
    alpha_mix = chol_solve(gram_mat, cross_mat)
    new_residual = residual_in - matmul_hi(image, alpha_mix)
    res_norms = jnp.sqrt(lax.optimization_barrier(jnp.sum(new_residual * new_residual, axis=0)) / POINTS)
    return (new_residual, res_norms)
```

```python
import functools

import jax
import jax.numpy as jnp
from jax import lax
from jax.experimental import pallas as pl
from jax.experimental.pallas import tpu as pltpu
from jax.sharding import PartitionSpec as P

ROW_LEVELS = 2
COL_LEVELS = 3


WAVENUM = 6.0
SOFTEN = 0.01
LANES = 128
SUB = 8
STREAMS = 2
MESH = pl.DeviceIdType.MESH


def from_behind(block, axis, distance):
    devices = range(lax.axis_size(axis))
    route = [(i - distance, i) for i in devices if i - distance in devices]
    return lax.ppermute(block, axis, route)


def from_partner(block, axis, distance):
    count = lax.axis_size(axis)
    route = []
    for low in range(count):
        high = low | 1 << distance
        if high != low and high < count:
            route += [(low, high), (high, low)]
    return lax.ppermute(block, axis, route)


def kernel_tile(own_xyz, other_xyz):
    dist_sq = (own_xyz[0][:, None] - other_xyz[0][None, :]) ** 2
    dist_sq = dist_sq + (own_xyz[1][:, None] - other_xyz[1][None, :]) ** 2
    dist_sq = dist_sq + (own_xyz[2][:, None] - other_xyz[2][None, :]) ** 2
    return jnp.cos(WAVENUM * jnp.sqrt(dist_sq)) / jnp.sqrt(dist_sq + SOFTEN)


def matmul_hi(left, right):
    return jnp.dot(
        left, right, precision=lax.Precision.HIGHEST, preferred_element_type=jnp.float32
    )


def inner_cols(left, right):
    return lax.dot_general(
        left,
        right,
        (((0,), (0,)), ((), ())),
        precision=lax.Precision.HIGHEST,
        preferred_element_type=jnp.float32,
    )


def pack_plan(width, devices):
    tiles = width // LANES
    gram_rows = tiles * (tiles + 1) // 2 * LANES
    cross_rows = tiles * width
    need = gram_rows + cross_rows + SUB
    unit = SUB * devices * STREAMS
    total = -(-need // unit) * unit
    return tiles, gram_rows, cross_rows, total


def gram_slots(tiles):
    return [(i, j) for i in range(tiles) for j in range(i, tiles)]


def bit_orders(n_row, n_col):
    col_bits = [("col", b) for b in range(n_col.bit_length() - 1)]
    row_bits = [("row", b) for b in range(n_row.bit_length() - 1)]
    core, side = col_bits[:1], col_bits[1:]
    first = core + side + row_bits
    second = core + row_bits[:1] + side + row_bits[1:]
    return first, second


def reduce_kernel(
    n_row, n_col, gram_ref, cross_ref, self_ref, out_ref, buf, land, full, rs_send, rs_recv, ag_send, ag_recv
):
    width = gram_ref.shape[0]
    tiles, gram_rows, cross_rows, total = pack_plan(width, n_row * n_col)
    place = {"row": lax.axis_index("row"), "col": lax.axis_index("col")}

    def bit_of(step):
        axis, b = step
        return place[axis] // (1 << b) % 2

    def partner_of(step):
        axis, b = step
        other = place[axis] + (1 - 2 * bit_of(step)) * (1 << b)
        if axis == "row":
            return (other, place["col"])
        return (place["row"], other)

    orders = bit_orders(n_row, n_col)
    barrier = pltpu.get_barrier_semaphore()
    for step in orders[0]:
        pl.semaphore_signal(barrier, inc=1, device_id=partner_of(step), device_id_type=MESH)

    for slot, (i, j) in enumerate(gram_slots(tiles)):
        buf[slot * LANES : (slot + 1) * LANES, :] = gram_ref[
            i * LANES : (i + 1) * LANES, j * LANES : (j + 1) * LANES
        ]
    for j in range(tiles):
        at = gram_rows + j * width
        buf[at : at + width, :] = cross_ref[:, j * LANES : (j + 1) * LANES]
    at = gram_rows + cross_rows
    buf[at:total, :] = jnp.zeros((total - at, LANES), jnp.float32)
    for j in range(tiles):
        buf[at + j : at + j + 1, :] = self_ref[:, j * LANES : (j + 1) * LANES]

    pl.semaphore_wait(barrier, len(orders[0]))

    share = total // STREAMS
    steps = len(orders[0])
    starts = [s * share for s in range(STREAMS)]
    history = []
    land_at = 0
    size = share
    for t in range(steps):
        half = size // 2
        copies = []
        keeps = []
        for s in range(STREAMS):
            step = orders[s][t]
            bit = bit_of(step)
            keep = pl.multiple_of(starts[s] + bit * half, SUB)
            give = pl.multiple_of(starts[s] + (1 - bit) * half, SUB)
            landing = land.at[pl.ds(s * share + land_at, half), :]
            copy = pltpu.make_async_remote_copy(
                src_ref=buf.at[pl.ds(give, half), :],
                dst_ref=landing,
                send_sem=rs_send.at[s, t],
                recv_sem=rs_recv.at[s, t],
                device_id=partner_of(step),
                device_id_type=MESH,
            )
            copy.start()
            copies.append(copy)
            keeps.append(keep)
        for s in range(STREAMS):
            copies[s].wait()
            here = pl.ds(keeps[s], half)
            buf[here, :] = buf[here, :] + land[s * share + land_at : s * share + land_at + half, :]
        history.append(keeps)
        starts = keeps
        land_at += half
        size = half
    for s in range(STREAMS):
        here = pl.ds(starts[s], size)
        full[here, :] = buf[here, :]
    for t in reversed(range(steps)):
        copies = []
        for s in range(STREAMS):
            here = pl.ds(history[t][s], size)
            copy = pltpu.make_async_remote_copy(
                src_ref=full.at[here, :],
                dst_ref=full.at[here, :],
                send_sem=ag_send.at[s, t],
                recv_sem=ag_recv.at[s, t],
                device_id=partner_of(orders[s][t]),
                device_id_type=MESH,
            )
            copy.start()
            copies.append(copy)
        for s in range(STREAMS):
            copies[s].wait()
        size = size * 2
    out_ref[...] = full[...]


def global_sum(gram_mat, cross_mat, self_squares):
    n_row, n_col = lax.axis_size("row"), lax.axis_size("col")
    width = gram_mat.shape[0]
    total = pack_plan(width, n_row * n_col)[-1]
    steps = len(bit_orders(n_row, n_col)[0])
    vmem = pl.BlockSpec(memory_space=pltpu.VMEM)
    return pl.pallas_call(
        functools.partial(reduce_kernel, n_row, n_col),
        out_shape=jax.ShapeDtypeStruct((total, LANES), jnp.float32),
        in_specs=[vmem] * 3,
        out_specs=vmem,
        scratch_shapes=[
            pltpu.VMEM((total, LANES), jnp.float32),
            pltpu.VMEM((total, LANES), jnp.float32),
            pltpu.VMEM((total, LANES), jnp.float32),
            pltpu.SemaphoreType.DMA((STREAMS, steps)),
            pltpu.SemaphoreType.DMA((STREAMS, steps)),
            pltpu.SemaphoreType.DMA((STREAMS, steps)),
            pltpu.SemaphoreType.DMA((STREAMS, steps)),
        ],
        compiler_params=pltpu.CompilerParams(collective_id=1, has_side_effects=True),
        name="sum_all",
    )(gram_mat, cross_mat, self_squares)


def invert_tile(tile):
    size = tile.shape[0]
    lane = lax.broadcasted_iota(jnp.int32, (SUB, size), 1)
    sub = lax.broadcasted_iota(jnp.int32, (SUB, size), 0)

    def panel(_, mat):
        top, rest = mat[:SUB], mat[SUB:]
        top_cols = [jnp.broadcast_to(top[:, m : m + 1], (SUB, size)) for m in range(SUB)]
        top = jnp.where(lane < SUB, 0.0, top)
        for i in range(SUB):
            pivot = jnp.broadcast_to(top_cols[i][i : i + 1], (SUB, size))
            inv = 1.0 / pivot
            own = sub == i
            factor = jnp.where(own, 0.0, top_cols[i])
            row = jnp.broadcast_to(top[i : i + 1], (SUB, size)) * inv
            row = jnp.where(lane == i, inv, row)
            top = jnp.where(own, row, top - factor * row)
            for m in range(i + 1, SUB):
                entry = jnp.broadcast_to(top_cols[m][i : i + 1], (SUB, size)) * inv
                top_cols[m] = jnp.where(own, entry, top_cols[m] - factor * entry)
        lane_rest = lax.broadcasted_iota(jnp.int32, rest.shape, 1)
        fresh = jnp.where(lane_rest < SUB, 0.0, rest)
        for m in range(SUB):
            fresh = fresh - jnp.broadcast_to(rest[:, m : m + 1], rest.shape) * top[m : m + 1]
        mat = jnp.concatenate([fresh, top], axis=0)
        return pltpu.roll(mat, size - SUB, 1)

    return lax.fori_loop(0, size // SUB, panel, tile)


def solve_kernel(points_total, packed_ref, image_ref, res_ref, new_ref, norm_ref, g_ref, c_ref):
    width = c_ref.shape[0]
    tiles = width // LANES
    gram_rows = tiles * (tiles + 1) // 2 * LANES
    for slot, (i, j) in enumerate(gram_slots(tiles)):
        g_ref[i * LANES : (i + 1) * LANES, j * LANES : (j + 1) * LANES] = packed_ref[
            slot * LANES : (slot + 1) * LANES, :
        ]
    for j in range(tiles):
        at = gram_rows + j * width
        c_ref[:, j * LANES : (j + 1) * LANES] = packed_ref[at : at + width, :]

    for k in range(tiles):
        lo, hi = k * LANES, (k + 1) * LANES
        inverse = invert_tile(g_ref[lo:hi, lo:hi])
        if hi < width:
            link = g_ref[lo:hi, hi:]
            right = matmul_hi(inverse, link)
            for i in range(k + 1, tiles):
                a, b = i * LANES, (i + 1) * LANES
                g_ref[a:b, a:] = g_ref[a:b, a:] - inner_cols(
                    link[:, a - hi : b - hi], right[:, a - hi :]
                )
            g_ref[lo:hi, hi:] = right
            mid = matmul_hi(inverse, c_ref[lo:hi, :])
            c_ref[lo:hi, :] = mid
            c_ref[hi:, :] = c_ref[hi:, :] - inner_cols(link, mid)
        else:
            c_ref[lo:hi, :] = matmul_hi(inverse, c_ref[lo:hi, :])
    for k in reversed(range(tiles - 1)):
        lo, hi = k * LANES, (k + 1) * LANES
        c_ref[lo:hi, :] = c_ref[lo:hi, :] - matmul_hi(g_ref[lo:hi, hi:], c_ref[hi:, :])

    new_ref[...] = res_ref[...] - matmul_hi(image_ref[...], c_ref[...])
    for j in range(tiles):
        at = gram_rows + j * width
        cols = slice(j * LANES, (j + 1) * LANES)
        explained = jnp.sum(c_ref[:, cols] * packed_ref[at : at + width, :], axis=0, keepdims=True)
        here = gram_rows + tiles * width + j
        left = packed_ref[here : here + 1, :] - explained
        norm_ref[:, cols] = jnp.sqrt(jnp.maximum(left, 0.0) / points_total)


def solve_step(packed, image, residual_in, points_total):
    width = residual_in.shape[1]
    vmem = pl.BlockSpec(memory_space=pltpu.VMEM)
    new_residual, norms = pl.pallas_call(
        functools.partial(solve_kernel, points_total),
        out_shape=(
            jax.ShapeDtypeStruct(residual_in.shape, jnp.float32),
            jax.ShapeDtypeStruct((1, width), jnp.float32),
        ),
        in_specs=[vmem] * 3,
        out_specs=(vmem, vmem),
        scratch_shapes=[
            pltpu.VMEM((width, width), jnp.float32),
            pltpu.VMEM((width, width), jnp.float32),
        ],
        name="solve_all",
    )(packed, image, residual_in)
    return new_residual, norms[0]


def shards(
    coords, residual_in, link_mask, compress, expand, level_gain, level_couple, partner_perm
):
    below_xyz, below_rhs = from_behind((coords, residual_in), ("row", "col"), 1)
    above_xyz, above_rhs = from_behind((coords, residual_in), ("row", "col"), -1)
    rank_width = compress.shape[1]
    coeffs = inner_cols(compress, residual_in)

    def mix_level(current, partner, level_at):
        taken_rows = partner_perm[0, level_at]
        picked = jnp.take(partner, taken_rows, axis=0)
        gain_col = level_gain[0, level_at * rank_width : (level_at + 1) * rank_width][:, None]
        couple = level_couple[:, level_at * rank_width : (level_at + 1) * rank_width]
        return gain_col * current + matmul_hi(couple, picked)

    row_top = lax.axis_size("row").bit_length() - 2
    for index_row in range(ROW_LEVELS):
        partner = from_partner(coeffs, "row", row_top - index_row)
        coeffs = mix_level(coeffs, partner, index_row)
    col_top = lax.axis_size("col").bit_length() - 2
    for index_col in range(COL_LEVELS):
        partner = from_partner(coeffs, "col", col_top - index_col)
        coeffs = mix_level(coeffs, partner, ROW_LEVELS + index_col)
    far_field = matmul_hi(expand, coeffs)
    weights = link_mask.astype(jnp.float32)
    near_scale = (3.0 * coords.shape[1]) ** (-0.5)
    near_field = matmul_hi(kernel_tile(coords, coords), residual_in)
    near_field = near_field + weights[0, 0] * matmul_hi(kernel_tile(coords, below_xyz), below_rhs)
    near_field = near_field + weights[0, 1] * matmul_hi(kernel_tile(coords, above_xyz), above_rhs)
    near_field = near_scale * near_field
    image = 2.0 * residual_in + near_field + far_field
    gram_mat = inner_cols(image, image)
    cross_mat = inner_cols(image, residual_in)
    points_total = coords.shape[1] * lax.axis_size("row") * lax.axis_size("col")
    self_squares = jnp.sum(residual_in * residual_in, axis=0)[None, :]
    packed = global_sum(gram_mat, cross_mat, self_squares)
    return solve_step(packed, image, residual_in, points_total)


def solution(mesh):
    return jax.shard_map(
        shards,
        mesh=mesh,
        in_specs=(
            P(None, ("row", "col")),
            P(("row", "col"), None),
            P(("row", "col"), None),
            P(("row", "col"), None),
            P(("row", "col"), None),
            P(("row", "col"), None),
            P(("row", "col"), None),
            P(("row", "col"), None, None),
        ),
        out_specs=(P(("row", "col"), None), P()),
        check_vma=False,
    )
```

```python
import functools

import jax
import jax.numpy as jnp
from jax import lax
from jax.experimental import pallas as pl
from jax.experimental.pallas import tpu as pltpu
from jax.sharding import PartitionSpec as P

ROW_LEVELS = 2
COL_LEVELS = 3


WAVENUM = 6.0
SOFTEN = 0.01
LANES = 128
SUB = 8
STREAMS = 2
MESH = pl.DeviceIdType.MESH


def kernel_tile(own_cols, other_rows):
    dist_sq = (own_cols[:, 0:1] - other_rows[0:1, :]) ** 2
    dist_sq = dist_sq + (own_cols[:, 1:2] - other_rows[1:2, :]) ** 2
    dist_sq = dist_sq + (own_cols[:, 2:3] - other_rows[2:3, :]) ** 2
    return jnp.cos(WAVENUM * jnp.sqrt(dist_sq)) / jnp.sqrt(dist_sq + SOFTEN)


def matmul_hi(left, right):
    return jnp.dot(
        left, right, precision=lax.Precision.HIGHEST, preferred_element_type=jnp.float32
    )


def inner_cols(left, right):
    return lax.dot_general(
        left,
        right,
        (((0,), (0,)), ((), ())),
        precision=lax.Precision.HIGHEST,
        preferred_element_type=jnp.float32,
    )


def pack_plan(width, devices):
    tiles = width // LANES
    gram_rows = tiles * (tiles + 1) // 2 * LANES
    cross_rows = tiles * width
    need = gram_rows + cross_rows + SUB
    unit = SUB * devices * STREAMS
    total = -(-need // unit) * unit
    return tiles, gram_rows, cross_rows, total


def gram_slots(tiles):
    return [(i, j) for i in range(tiles) for j in range(i, tiles)]


def bit_orders(n_row, n_col):
    col_bits = [("col", b) for b in range(n_col.bit_length() - 1)]
    row_bits = [("row", b) for b in range(n_row.bit_length() - 1)]
    core, side = col_bits[:1], col_bits[1:]
    first = core + side + row_bits
    second = core + row_bits[:1] + side + row_bits[1:]
    return first, second


def reduce_kernel(
    n_row, n_col, image_ref, res_ref, out_ref, buf, land, full, rs_send, rs_recv, ag_send, ag_recv
):
    width = image_ref.shape[1]
    tiles, gram_rows, cross_rows, total = pack_plan(width, n_row * n_col)
    place = {"row": lax.axis_index("row"), "col": lax.axis_index("col")}

    def bit_of(step):
        axis, b = step
        return place[axis] // (1 << b) % 2

    def partner_of(step):
        axis, b = step
        other = place[axis] + (1 - 2 * bit_of(step)) * (1 << b)
        if axis == "row":
            return (other, place["col"])
        return (place["row"], other)

    orders = bit_orders(n_row, n_col)
    barrier = pltpu.get_barrier_semaphore()
    for step in orders[0]:
        pl.semaphore_signal(barrier, inc=1, device_id=partner_of(step), device_id_type=MESH)

    slot = 0
    for i in range(tiles):
        rows = inner_cols(image_ref[:, i * LANES : (i + 1) * LANES], image_ref[:, i * LANES :])
        for j in range(tiles - i):
            at = slot * LANES
            buf[at : at + LANES, :] = rows[:, j * LANES : (j + 1) * LANES]
            slot += 1
    for i in range(tiles):
        rows = inner_cols(image_ref[:, i * LANES : (i + 1) * LANES], res_ref[...])
        for j in range(tiles):
            at = gram_rows + j * width + i * LANES
            buf[at : at + LANES, :] = rows[:, j * LANES : (j + 1) * LANES]
    at = gram_rows + cross_rows
    buf[at:total, :] = jnp.zeros((total - at, LANES), jnp.float32)
    squares = jnp.sum(res_ref[...] * res_ref[...], axis=0, keepdims=True)
    for j in range(tiles):
        buf[at + j : at + j + 1, :] = squares[:, j * LANES : (j + 1) * LANES]

    pl.semaphore_wait(barrier, len(orders[0]))

    share = total // STREAMS
    steps = len(orders[0])
    starts = [s * share for s in range(STREAMS)]
    history = []
    land_at = 0
    size = share
    for t in range(steps):
        half = size // 2
        copies = []
        keeps = []
        for s in range(STREAMS):
            step = orders[s][t]
            bit = bit_of(step)
            keep = pl.multiple_of(starts[s] + bit * half, SUB)
            give = pl.multiple_of(starts[s] + (1 - bit) * half, SUB)
            landing = land.at[pl.ds(s * share + land_at, half), :]
            copy = pltpu.make_async_remote_copy(
                src_ref=buf.at[pl.ds(give, half), :],
                dst_ref=landing,
                send_sem=rs_send.at[s, t],
                recv_sem=rs_recv.at[s, t],
                device_id=partner_of(step),
                device_id_type=MESH,
            )
            copy.start()
            copies.append(copy)
            keeps.append(keep)
        for s in range(STREAMS):
            copies[s].wait()
            here = pl.ds(keeps[s], half)
            buf[here, :] = buf[here, :] + land[s * share + land_at : s * share + land_at + half, :]
        history.append(keeps)
        starts = keeps
        land_at += half
        size = half
    for s in range(STREAMS):
        here = pl.ds(starts[s], size)
        full[here, :] = buf[here, :]
    for t in reversed(range(steps)):
        copies = []
        for s in range(STREAMS):
            here = pl.ds(history[t][s], size)
            copy = pltpu.make_async_remote_copy(
                src_ref=full.at[here, :],
                dst_ref=full.at[here, :],
                send_sem=ag_send.at[s, t],
                recv_sem=ag_recv.at[s, t],
                device_id=partner_of(orders[s][t]),
                device_id_type=MESH,
            )
            copy.start()
            copies.append(copy)
        for s in range(STREAMS):
            copies[s].wait()
        size = size * 2
    out_ref[...] = full[...]


def global_sum(image, residual_in):
    n_row, n_col = lax.axis_size("row"), lax.axis_size("col")
    width = image.shape[1]
    total = pack_plan(width, n_row * n_col)[-1]
    steps = len(bit_orders(n_row, n_col)[0])
    vmem = pl.BlockSpec(memory_space=pltpu.VMEM)
    return pl.pallas_call(
        functools.partial(reduce_kernel, n_row, n_col),
        out_shape=jax.ShapeDtypeStruct((total, LANES), jnp.float32),
        in_specs=[vmem] * 2,
        out_specs=vmem,
        scratch_shapes=[
            pltpu.VMEM((total, LANES), jnp.float32),
            pltpu.VMEM((total, LANES), jnp.float32),
            pltpu.VMEM((total, LANES), jnp.float32),
            pltpu.SemaphoreType.DMA((STREAMS, steps)),
            pltpu.SemaphoreType.DMA((STREAMS, steps)),
            pltpu.SemaphoreType.DMA((STREAMS, steps)),
            pltpu.SemaphoreType.DMA((STREAMS, steps)),
        ],
        compiler_params=pltpu.CompilerParams(collective_id=1, has_side_effects=True),
        name="sum_all",
    )(image, residual_in)


def invert_tile(tile):
    size = tile.shape[0]
    lane = lax.broadcasted_iota(jnp.int32, (SUB, size), 1)
    sub = lax.broadcasted_iota(jnp.int32, (SUB, size), 0)

    def panel(_, mat):
        top, rest = mat[:SUB], mat[SUB:]
        top_cols = [jnp.broadcast_to(top[:, m : m + 1], (SUB, size)) for m in range(SUB)]
        top = jnp.where(lane < SUB, 0.0, top)
        for i in range(SUB):
            pivot = jnp.broadcast_to(top_cols[i][i : i + 1], (SUB, size))
            inv = 1.0 / pivot
            own = sub == i
            factor = jnp.where(own, 0.0, top_cols[i])
            row = jnp.broadcast_to(top[i : i + 1], (SUB, size)) * inv
            row = jnp.where(lane == i, inv, row)
            top = jnp.where(own, row, top - factor * row)
            for m in range(i + 1, SUB):
                entry = jnp.broadcast_to(top_cols[m][i : i + 1], (SUB, size)) * inv
                top_cols[m] = jnp.where(own, entry, top_cols[m] - factor * entry)
        lane_rest = lax.broadcasted_iota(jnp.int32, rest.shape, 1)
        fresh = jnp.where(lane_rest < SUB, 0.0, rest)
        for m in range(SUB):
            fresh = fresh - jnp.broadcast_to(rest[:, m : m + 1], rest.shape) * top[m : m + 1]
        mat = jnp.concatenate([fresh, top], axis=0)
        return pltpu.roll(mat, size - SUB, 1)

    return lax.fori_loop(0, size // SUB, panel, tile)


def solve_kernel(points_total, packed_ref, image_ref, res_ref, new_ref, norm_ref, g_ref, c_ref):
    width = c_ref.shape[0]
    tiles = width // LANES
    gram_rows = tiles * (tiles + 1) // 2 * LANES
    for slot, (i, j) in enumerate(gram_slots(tiles)):
        g_ref[i * LANES : (i + 1) * LANES, j * LANES : (j + 1) * LANES] = packed_ref[
            slot * LANES : (slot + 1) * LANES, :
        ]
    for j in range(tiles):
        at = gram_rows + j * width
        c_ref[:, j * LANES : (j + 1) * LANES] = packed_ref[at : at + width, :]

    for k in range(tiles):
        lo, hi = k * LANES, (k + 1) * LANES
        inverse = invert_tile(g_ref[lo:hi, lo:hi])
        if hi < width:
            link = g_ref[lo:hi, hi:]
            right = matmul_hi(inverse, link)
            for i in range(k + 1, tiles):
                a, b = i * LANES, (i + 1) * LANES
                g_ref[a:b, a:] = g_ref[a:b, a:] - inner_cols(
                    link[:, a - hi : b - hi], right[:, a - hi :]
                )
            g_ref[lo:hi, hi:] = right
            mid = matmul_hi(inverse, c_ref[lo:hi, :])
            c_ref[lo:hi, :] = mid
            c_ref[hi:, :] = c_ref[hi:, :] - inner_cols(link, mid)
        else:
            c_ref[lo:hi, :] = matmul_hi(inverse, c_ref[lo:hi, :])
    for k in reversed(range(tiles - 1)):
        lo, hi = k * LANES, (k + 1) * LANES
        c_ref[lo:hi, :] = c_ref[lo:hi, :] - matmul_hi(g_ref[lo:hi, hi:], c_ref[hi:, :])

    new_ref[...] = res_ref[...] - matmul_hi(image_ref[...], c_ref[...])
    for j in range(tiles):
        at = gram_rows + j * width
        cols = slice(j * LANES, (j + 1) * LANES)
        explained = jnp.sum(c_ref[:, cols] * packed_ref[at : at + width, :], axis=0, keepdims=True)
        here = gram_rows + tiles * width + j
        left = packed_ref[here : here + 1, :] - explained
        norm_ref[:, cols] = jnp.sqrt(jnp.maximum(left, 0.0) / points_total)


def solve_step(packed, image, residual_in, points_total):
    width = residual_in.shape[1]
    vmem = pl.BlockSpec(memory_space=pltpu.VMEM)
    new_residual, norms = pl.pallas_call(
        functools.partial(solve_kernel, points_total),
        out_shape=(
            jax.ShapeDtypeStruct(residual_in.shape, jnp.float32),
            jax.ShapeDtypeStruct((1, width), jnp.float32),
        ),
        in_specs=[vmem] * 3,
        out_specs=(vmem, vmem),
        scratch_shapes=[
            pltpu.VMEM((width, width), jnp.float32),
            pltpu.VMEM((width, width), jnp.float32),
        ],
        name="solve_all",
    )(packed, image, residual_in)
    return new_residual, norms[0]


def image_kernel(
    n_row, n_col,
    coords_ref, points_ref, res_ref, mask_ref, comp_ref, exp_ref, gain_ref, couple_ref, perm_ref,
    image_ref,
    mixed, gains, coef, land, land_res, land_comp, halo_res, halo_xyz,
    comp_sems, res_sems, halo_sems, xyz_sems, level_sems,
):
    rank = comp_ref.shape[1]
    width = res_ref.shape[1]
    chunks = width // LANES
    levels = ROW_LEVELS + COL_LEVELS
    at_row, at_col = lax.axis_index("row"), lax.axis_index("col")
    group = at_row * n_col + at_col
    has_side = (group > 0, group < n_row * n_col - 1)

    def partner_of(level):
        if level < ROW_LEVELS:
            bit = n_row.bit_length() - 2 - level
            return (at_row + (1 - 2 * (at_row // (1 << bit) % 2)) * (1 << bit), at_col)
        bit = n_col.bit_length() - 2 - (level - ROW_LEVELS)
        return (at_row, at_col + (1 - 2 * (at_col // (1 << bit) % 2)) * (1 << bit))

    def beside(side):
        other = group + (2 * side - 1)
        return (other // n_col, other % n_col)

    def remote(src, dst, sems, where):
        return pltpu.make_async_remote_copy(
            src_ref=src,
            dst_ref=dst,
            send_sem=sems.at[0],
            recv_sem=sems.at[1],
            device_id=where,
            device_id_type=MESH,
        )

    barrier = pltpu.get_barrier_semaphore()
    for level in range(levels):
        pl.semaphore_signal(barrier, inc=1, device_id=partner_of(level), device_id_type=MESH)
    for side in range(2):
        @pl.when(has_side[side])
        def _():
            pl.semaphore_signal(barrier, inc=1, device_id=beside(side), device_id_type=MESH)
    sides = jnp.minimum(group, 1) + jnp.minimum(n_row * n_col - 1 - group, 1)
    pl.semaphore_wait(barrier, levels + sides)

    def cols(k):
        return pl.ds(k * LANES, LANES)

    comp_copy = remote(comp_ref, land_comp, comp_sems, partner_of(0))
    comp_copy.start()
    res_copies = []
    for k in range(chunks):
        copy = remote(res_ref.at[:, cols(k)], land_res.at[k], res_sems.at[k], partner_of(0))
        copy.start()
        res_copies.append(copy)
    halo_copies = [
        (
            remote(coords_ref, halo_xyz.at[1 - side], xyz_sems.at[side], beside(side)),
            remote(res_ref, halo_res.at[1 - side], halo_sems.at[side], beside(side)),
        )
        for side in range(2)
    ]
    halo_waits = [
        (
            remote(coords_ref, halo_xyz.at[side], xyz_sems.at[1 - side], beside(side)),
            remote(res_ref, halo_res.at[side], halo_sems.at[1 - side], beside(side)),
        )
        for side in range(2)
    ]
    for side in range(2):
        @pl.when(has_side[side])
        def _():
            halo_copies[side][0].start()
            halo_copies[side][1].start()

        @pl.when(jnp.logical_not(has_side[side]))
        def _():
            halo_xyz[side] = jnp.zeros(halo_xyz.shape[1:], jnp.float32)
            halo_res[side] = jnp.zeros(halo_res.shape[1:], jnp.float32)

    down = lax.broadcasted_iota(jnp.int32, (rank, rank), 0)
    across = lax.broadcasted_iota(jnp.int32, (rank, rank), 1)
    for level in range(levels):
        here = slice(level * rank, (level + 1) * rank)
        taken = jnp.where(down == perm_ref[0, level : level + 1, :], 1.0, 0.0)
        mixed[level] = lax.dot_general(
            couple_ref[:, here],
            taken,
            (((1,), (1,)), ((), ())),
            precision=lax.Precision.HIGHEST,
            preferred_element_type=jnp.float32,
        )
        spread = jnp.where(down == across, gain_ref[:, here], 0.0)
        gains[level] = jnp.broadcast_to(jnp.sum(spread, axis=1, keepdims=True), (rank, LANES))

    own = inner_cols(comp_ref[...], res_ref[...])
    near_scale = (3.0 * res_ref.shape[0]) ** (-0.5)
    own_tile = near_scale * kernel_tile(points_ref[...], coords_ref[...])
    image_ref[...] = 2.0 * res_ref[...] + matmul_hi(own_tile, res_ref[...])

    comp_copy.wait()
    first = lax.dot_general(
        mixed[0],
        land_comp[...],
        (((1,), (1,)), ((), ())),
        precision=lax.Precision.HIGHEST,
        preferred_element_type=jnp.float32,
    )

    copies = {}

    def step(level, k):
        if level == 0:
            res_copies[k].wait()
            fresh = gains[0] * own[:, k * LANES : (k + 1) * LANES] + matmul_hi(first, land_res[k])
        else:
            copies[level, k].wait()
            fresh = gains[level] * coef[level - 1, k] + matmul_hi(mixed[level], land[level - 1, k])
        if level == levels - 1:
            image_ref[:, cols(k)] = image_ref[:, cols(k)] + matmul_hi(exp_ref[...], fresh)
            return
        coef[level, k] = fresh
        copy = remote(coef.at[level, k], land.at[level, k], level_sems.at[level, k], partner_of(level + 1))
        copy.start()
        copies[level + 1, k] = copy

    def near_side(side):
        @pl.when(has_side[side])
        def _():
            for copy in halo_copies[side]:
                copy.wait_send()
            for copy in halo_waits[side]:
                copy.wait_recv()

        keep = mask_ref[0:1, side : side + 1].astype(jnp.float32) * near_scale
        tile = keep * kernel_tile(points_ref[...], halo_xyz[side])
        image_ref[...] = image_ref[...] + matmul_hi(tile, halo_res[side])

    for wave in range(levels + chunks - 1):
        for level in reversed(range(levels)):
            if 0 <= wave - level < chunks:
                step(level, wave - level)
        if wave == chunks - 1:
            near_side(0)
        if wave == chunks:
            near_side(1)


def local_image(
    coords, residual_in, link_mask, compress, expand, level_gain, level_couple, partner_perm
):
    n_row, n_col = lax.axis_size("row"), lax.axis_size("col")
    points, width = residual_in.shape
    rank = compress.shape[1]
    chunks = width // LANES
    levels = ROW_LEVELS + COL_LEVELS
    vmem = pl.BlockSpec(memory_space=pltpu.VMEM)
    dma = pltpu.SemaphoreType.DMA
    f32 = jnp.float32
    return pl.pallas_call(
        functools.partial(image_kernel, n_row, n_col),
        out_shape=jax.ShapeDtypeStruct((points, width), f32),
        in_specs=[vmem] * 9,
        out_specs=vmem,
        scratch_shapes=[
            pltpu.VMEM((levels, rank, rank), f32),
            pltpu.VMEM((levels, rank, LANES), f32),
            pltpu.VMEM((levels - 1, chunks, rank, LANES), f32),
            pltpu.VMEM((levels - 1, chunks, rank, LANES), f32),
            pltpu.VMEM((chunks, points, LANES), f32),
            pltpu.VMEM((points, rank), f32),
            pltpu.VMEM((2, points, width), f32),
            pltpu.VMEM((2, coords.shape[0], points), f32),
            dma((2,)),
            dma((chunks, 2)),
            dma((2, 2)),
            dma((2, 2)),
            dma((levels - 1, chunks, 2)),
        ],
        compiler_params=pltpu.CompilerParams(collective_id=2, has_side_effects=True),
        name="image_all",
    )(
        coords, coords.T, residual_in, link_mask, compress, expand, level_gain, level_couple,
        partner_perm,
    )


def shards(
    coords, residual_in, link_mask, compress, expand, level_gain, level_couple, partner_perm
):
    image = local_image(
        coords, residual_in, link_mask, compress, expand, level_gain, level_couple, partner_perm
    )
    points_total = coords.shape[1] * lax.axis_size("row") * lax.axis_size("col")
    packed = global_sum(image, residual_in)
    return solve_step(packed, image, residual_in, points_total)


def solution(mesh):
    return jax.shard_map(
        shards,
        mesh=mesh,
        in_specs=(
            P(None, ("row", "col")),
            P(("row", "col"), None),
            P(("row", "col"), None),
            P(("row", "col"), None),
            P(("row", "col"), None),
            P(("row", "col"), None),
            P(("row", "col"), None),
            P(("row", "col"), None, None),
        ),
        out_specs=(P(("row", "col"), None), P()),
        check_vma=False,
    )
```

```python
import functools

import jax
import jax.numpy as jnp
from jax import lax
from jax.experimental import pallas as pl
from jax.experimental.pallas import tpu as pltpu
from jax.sharding import PartitionSpec as P

ROW_LEVELS = 2
COL_LEVELS = 3


WAVENUM = 6.0
SOFTEN = 0.01
LANES = 128
SUB = 8
GRAM_STREAMS = 3
CROSS_STREAMS = 2
MESH = pl.DeviceIdType.MESH


def kernel_tile(own_cols, other_rows):
    dist_sq = (own_cols[:, 0:1] - other_rows[0:1, :]) ** 2
    dist_sq = dist_sq + (own_cols[:, 1:2] - other_rows[1:2, :]) ** 2
    dist_sq = dist_sq + (own_cols[:, 2:3] - other_rows[2:3, :]) ** 2
    return jnp.cos(WAVENUM * jnp.sqrt(dist_sq)) / jnp.sqrt(dist_sq + SOFTEN)


def matmul_hi(left, right):
    return jnp.dot(
        left, right, precision=lax.Precision.HIGHEST, preferred_element_type=jnp.float32
    )


def inner_cols(left, right):
    return lax.dot_general(
        left,
        right,
        (((0,), (0,)), ((), ())),
        precision=lax.Precision.HIGHEST,
        preferred_element_type=jnp.float32,
    )


def padded(rows, devices, streams):
    unit = SUB * devices * streams
    return -(-rows // unit) * unit


def gram_slots(tiles):
    return [(i, j) for i in range(tiles) for j in range(i, tiles)]


def stream_orders(n_row, n_col, streams):
    col_bits = [("col", b) for b in range(n_col.bit_length() - 1)]
    row_bits = [("row", b) for b in range(n_row.bit_length() - 1)]
    lead = col_bits[1:] + row_bits[:1]
    tail = col_bits[:1] + row_bits[1:]
    return [lead[s:] + lead[:s] + tail for s in range(streams)]


def bit_of(step):
    axis, b = step
    return lax.axis_index(axis) // (1 << b) % 2


def flipped(step):
    axis, b = step
    place = {"row": lax.axis_index("row"), "col": lax.axis_index("col")}
    place[axis] = place[axis] + (1 - 2 * bit_of(step)) * (1 << b)
    return (place["row"], place["col"])


def sum_phases(orders, buf, land, full, rs_send, rs_recv, ag_send, ag_recv):
    streams, steps = len(orders), len(orders[0])
    share = buf.shape[0] // streams
    starts = [s * share for s in range(streams)]
    history = []
    land_at = 0
    size = share
    for t in range(steps):
        half = size // 2
        copies = []
        keeps = []
        for s in range(streams):
            step = orders[s][t]
            bit = bit_of(step)
            keeps.append(pl.multiple_of(starts[s] + bit * half, SUB))
            give = pl.multiple_of(starts[s] + (1 - bit) * half, SUB)
            copy = pltpu.make_async_remote_copy(
                src_ref=buf.at[pl.ds(give, half), :],
                dst_ref=land.at[pl.ds(s * share + land_at, half), :],
                send_sem=rs_send.at[s, t],
                recv_sem=rs_recv.at[s, t],
                device_id=flipped(step),
                device_id_type=MESH,
            )
            copy.start()
            copies.append(copy)
        yield
        for s in range(streams):
            copies[s].wait()
            here = pl.ds(keeps[s], half)
            got = land[s * share + land_at : s * share + land_at + half, :]
            if t == steps - 1:
                full[here, :] = buf[here, :] + got
            else:
                buf[here, :] = buf[here, :] + got
        history.append(keeps)
        starts = keeps
        land_at += half
        size = half
    for t in reversed(range(steps)):
        copies = []
        for s in range(streams):
            here = full.at[pl.ds(history[t][s], size), :]
            copy = pltpu.make_async_remote_copy(
                src_ref=here,
                dst_ref=here,
                send_sem=ag_send.at[s, t],
                recv_sem=ag_recv.at[s, t],
                device_id=flipped(orders[s][t]),
                device_id_type=MESH,
            )
            copy.start()
            copies.append(copy)
        yield
        for copy in copies:
            copy.wait()
        size = size * 2


def invert_panels(tile, count):
    size = tile.shape[0]
    lane = lax.broadcasted_iota(jnp.int32, (SUB, size), 1)
    sub = lax.broadcasted_iota(jnp.int32, (SUB, size), 0)

    def panel(_, mat):
        top, rest = mat[:SUB], mat[SUB:]
        top_cols = [jnp.broadcast_to(top[:, m : m + 1], (SUB, size)) for m in range(SUB)]
        top = jnp.where(lane < SUB, 0.0, top)
        for i in range(SUB):
            pivot = jnp.broadcast_to(top_cols[i][i : i + 1], (SUB, size))
            inv = 1.0 / pivot
            own = sub == i
            factor = jnp.where(own, 0.0, top_cols[i])
            row = jnp.broadcast_to(top[i : i + 1], (SUB, size)) * inv
            row = jnp.where(lane == i, inv, row)
            top = jnp.where(own, row, top - factor * row)
            for m in range(i + 1, SUB):
                entry = jnp.broadcast_to(top_cols[m][i : i + 1], (SUB, size)) * inv
                top_cols[m] = jnp.where(own, entry, top_cols[m] - factor * entry)
        lane_rest = lax.broadcasted_iota(jnp.int32, rest.shape, 1)
        fresh = jnp.where(lane_rest < SUB, 0.0, rest)
        for m in range(SUB):
            fresh = fresh - jnp.broadcast_to(rest[:, m : m + 1], rest.shape) * top[m : m + 1]
        mat = jnp.concatenate([fresh, top], axis=0)
        return pltpu.roll(mat, size - SUB, 1)

    return lax.fori_loop(0, count, panel, tile)


def finish_kernel(
    n_row, n_col, image_ref, res_ref, new_ref, norm_ref,
    g_buf, g_land, g_full, c_buf, c_land, c_full, g_ref, c_ref, inv_ref, *sems
):
    width = image_ref.shape[1]
    tiles = width // LANES
    points_total = image_ref.shape[0] * n_row * n_col
    gram_rows = tiles * (tiles + 1) // 2 * LANES
    g_orders = stream_orders(n_row, n_col, GRAM_STREAMS)
    c_orders = stream_orders(n_row, n_col, CROSS_STREAMS)

    barrier = pltpu.get_barrier_semaphore()
    for step in g_orders[0]:
        pl.semaphore_signal(barrier, inc=1, device_id=flipped(step), device_id_type=MESH)

    slot = 0
    for i in range(tiles):
        rows = inner_cols(image_ref[:, i * LANES : (i + 1) * LANES], image_ref[:, i * LANES :])
        for j in range(tiles - i):
            at = slot * LANES
            g_buf[at : at + LANES, :] = rows[:, j * LANES : (j + 1) * LANES]
            slot += 1
    g_buf[gram_rows:, :] = jnp.zeros((g_buf.shape[0] - gram_rows, LANES), jnp.float32)
    squares = jnp.sum(res_ref[...] * res_ref[...], axis=0, keepdims=True)
    for j in range(tiles):
        g_buf[gram_rows + j : gram_rows + j + 1, :] = squares[:, j * LANES : (j + 1) * LANES]

    pl.semaphore_wait(barrier, len(g_orders[0]))
    gram_sum = sum_phases(g_orders, g_buf, g_land, g_full, *sems[:4])
    next(gram_sum)
    for i in range(tiles):
        rows = inner_cols(image_ref[:, i * LANES : (i + 1) * LANES], res_ref[...])
        for j in range(tiles):
            at = j * width + i * LANES
            c_buf[at : at + LANES, :] = rows[:, j * LANES : (j + 1) * LANES]
    spare = c_buf.shape[0] - tiles * width
    if spare:
        c_buf[tiles * width :, :] = jnp.zeros((spare, LANES), jnp.float32)
    for _ in gram_sum:
        pass
    cross_sum = sum_phases(c_orders, c_buf, c_land, c_full, *sems[4:])
    next(cross_sum)

    for slot, (i, j) in enumerate(gram_slots(tiles)):
        g_ref[i * LANES : (i + 1) * LANES, j * LANES : (j + 1) * LANES] = g_full[
            slot * LANES : (slot + 1) * LANES, :
        ]
    panels = LANES // SUB
    for k in range(tiles):
        lo, hi = k * LANES, (k + 1) * LANES
        inverse = invert_panels(g_ref[lo:hi, lo:hi], panels // 2)
        next(cross_sum, None)
        inverse = invert_panels(inverse, panels - panels // 2)
        inv_ref[lo:hi, :] = inverse
        next(cross_sum, None)
        if hi < width:
            link = g_ref[lo:hi, hi:]
            right = matmul_hi(inverse, link)
            for i in range(k + 1, tiles):
                a, b = i * LANES, (i + 1) * LANES
                g_ref[a:b, a:] = g_ref[a:b, a:] - inner_cols(
                    link[:, a - hi : b - hi], right[:, a - hi :]
                )
            g_ref[lo:hi, hi:] = right
            next(cross_sum, None)
    for _ in cross_sum:
        pass

    for j in range(tiles):
        c_ref[:, j * LANES : (j + 1) * LANES] = c_full[j * width : (j + 1) * width, :]
    for k in range(tiles):
        lo, hi = k * LANES, (k + 1) * LANES
        part = c_ref[lo:hi, :]
        c_ref[lo:hi, :] = matmul_hi(inv_ref[lo:hi, :], part)
        if hi < width:
            c_ref[hi:, :] = c_ref[hi:, :] - inner_cols(g_ref[lo:hi, hi:], part)
    for k in reversed(range(tiles - 1)):
        lo, hi = k * LANES, (k + 1) * LANES
        c_ref[lo:hi, :] = c_ref[lo:hi, :] - matmul_hi(g_ref[lo:hi, hi:], c_ref[hi:, :])

    new_ref[...] = res_ref[...] - matmul_hi(image_ref[...], c_ref[...])
    for j in range(tiles):
        cols = slice(j * LANES, (j + 1) * LANES)
        cross = c_full[j * width : (j + 1) * width, :]
        explained = jnp.sum(c_ref[:, cols] * cross, axis=0, keepdims=True)
        left = g_full[gram_rows + j : gram_rows + j + 1, :] - explained
        norm_ref[:, cols] = jnp.sqrt(jnp.maximum(left, 0.0) / points_total)


def finish_step(image, residual_in):
    n_row, n_col = lax.axis_size("row"), lax.axis_size("col")
    width = residual_in.shape[1]
    tiles = width // LANES
    gram_total = padded(tiles * (tiles + 1) // 2 * LANES + SUB, n_row * n_col, GRAM_STREAMS)
    cross_total = padded(tiles * width, n_row * n_col, CROSS_STREAMS)
    steps = len(stream_orders(n_row, n_col, 1)[0])
    vmem = pl.BlockSpec(memory_space=pltpu.VMEM)
    new_residual, norms = pl.pallas_call(
        functools.partial(finish_kernel, n_row, n_col),
        out_shape=(
            jax.ShapeDtypeStruct(residual_in.shape, jnp.float32),
            jax.ShapeDtypeStruct((1, width), jnp.float32),
        ),
        in_specs=[vmem] * 2,
        out_specs=(vmem, vmem),
        scratch_shapes=[pltpu.VMEM((gram_total, LANES), jnp.float32)] * 3
        + [pltpu.VMEM((cross_total, LANES), jnp.float32)] * 3
        + [pltpu.VMEM((width, width), jnp.float32)] * 2
        + [pltpu.VMEM((width, LANES), jnp.float32)]
        + [pltpu.SemaphoreType.DMA((GRAM_STREAMS, steps))] * 4
        + [pltpu.SemaphoreType.DMA((CROSS_STREAMS, steps))] * 4,
        compiler_params=pltpu.CompilerParams(collective_id=1, has_side_effects=True),
        name="finish_all",
    )(image, residual_in)
    return new_residual, norms[0]


def image_kernel(
    n_row, n_col,
    coords_ref, points_ref, res_ref, mask_ref, comp_ref, exp_ref, gain_ref, couple_ref, perm_ref,
    image_ref,
    mixed, gains, coef, land, land_res, land_comp, halo_res, halo_xyz,
    comp_sems, res_sems, halo_sems, xyz_sems, level_sems,
):
    rank = comp_ref.shape[1]
    width = res_ref.shape[1]
    chunks = width // LANES
    levels = ROW_LEVELS + COL_LEVELS
    at_row, at_col = lax.axis_index("row"), lax.axis_index("col")
    group = at_row * n_col + at_col
    has_side = (group > 0, group < n_row * n_col - 1)

    def partner_of(level):
        if level < ROW_LEVELS:
            bit = n_row.bit_length() - 2 - level
            return (at_row + (1 - 2 * (at_row // (1 << bit) % 2)) * (1 << bit), at_col)
        bit = n_col.bit_length() - 2 - (level - ROW_LEVELS)
        return (at_row, at_col + (1 - 2 * (at_col // (1 << bit) % 2)) * (1 << bit))

    def beside(side):
        other = group + (2 * side - 1)
        return (other // n_col, other % n_col)

    def remote(src, dst, sems, where):
        return pltpu.make_async_remote_copy(
            src_ref=src,
            dst_ref=dst,
            send_sem=sems.at[0],
            recv_sem=sems.at[1],
            device_id=where,
            device_id_type=MESH,
        )

    barrier = pltpu.get_barrier_semaphore()
    for level in range(levels):
        pl.semaphore_signal(barrier, inc=1, device_id=partner_of(level), device_id_type=MESH)
    for side in range(2):
        @pl.when(has_side[side])
        def _():
            pl.semaphore_signal(barrier, inc=1, device_id=beside(side), device_id_type=MESH)
    sides = jnp.minimum(group, 1) + jnp.minimum(n_row * n_col - 1 - group, 1)
    pl.semaphore_wait(barrier, levels + sides)

    def cols(k):
        return pl.ds(k * LANES, LANES)

    comp_copy = remote(comp_ref, land_comp, comp_sems, partner_of(0))
    comp_copy.start()
    res_copies = []
    for k in range(chunks):
        copy = remote(res_ref.at[:, cols(k)], land_res.at[k], res_sems.at[k], partner_of(0))
        copy.start()
        res_copies.append(copy)
    halo_copies = [
        (
            remote(coords_ref, halo_xyz.at[1 - side], xyz_sems.at[side], beside(side)),
            remote(res_ref, halo_res.at[1 - side], halo_sems.at[side], beside(side)),
        )
        for side in range(2)
    ]
    halo_waits = [
        (
            remote(coords_ref, halo_xyz.at[side], xyz_sems.at[1 - side], beside(side)),
            remote(res_ref, halo_res.at[side], halo_sems.at[1 - side], beside(side)),
        )
        for side in range(2)
    ]
    for side in range(2):
        @pl.when(has_side[side])
        def _():
            halo_copies[side][0].start()
            halo_copies[side][1].start()

        @pl.when(jnp.logical_not(has_side[side]))
        def _():
            halo_xyz[side] = jnp.zeros(halo_xyz.shape[1:], jnp.float32)
            halo_res[side] = jnp.zeros(halo_res.shape[1:], jnp.float32)

    down = lax.broadcasted_iota(jnp.int32, (rank, rank), 0)
    across = lax.broadcasted_iota(jnp.int32, (rank, rank), 1)
    for level in range(levels):
        here = slice(level * rank, (level + 1) * rank)
        taken = jnp.where(down == perm_ref[0, level : level + 1, :], 1.0, 0.0)
        mixed[level] = lax.dot_general(
            couple_ref[:, here],
            taken,
            (((1,), (1,)), ((), ())),
            precision=lax.Precision.HIGHEST,
            preferred_element_type=jnp.float32,
        )
        spread = jnp.where(down == across, gain_ref[:, here], 0.0)
        gains[level] = jnp.broadcast_to(jnp.sum(spread, axis=1, keepdims=True), (rank, LANES))

    own = inner_cols(comp_ref[...], res_ref[...])
    near_scale = (3.0 * res_ref.shape[0]) ** (-0.5)
    own_tile = near_scale * kernel_tile(points_ref[...], coords_ref[...])
    image_ref[...] = 2.0 * res_ref[...] + matmul_hi(own_tile, res_ref[...])

    comp_copy.wait()
    first = lax.dot_general(
        mixed[0],
        land_comp[...],
        (((1,), (1,)), ((), ())),
        precision=lax.Precision.HIGHEST,
        preferred_element_type=jnp.float32,
    )

    copies = {}

    def step(level, k):
        if level == 0:
            res_copies[k].wait()
            fresh = gains[0] * own[:, k * LANES : (k + 1) * LANES] + matmul_hi(first, land_res[k])
        else:
            copies[level, k].wait()
            fresh = gains[level] * coef[level - 1, k] + matmul_hi(mixed[level], land[level - 1, k])
        if level == levels - 1:
            image_ref[:, cols(k)] = image_ref[:, cols(k)] + matmul_hi(exp_ref[...], fresh)
            return
        coef[level, k] = fresh
        copy = remote(coef.at[level, k], land.at[level, k], level_sems.at[level, k], partner_of(level + 1))
        copy.start()
        copies[level + 1, k] = copy

    def near_side(side):
        @pl.when(has_side[side])
        def _():
            for copy in halo_copies[side]:
                copy.wait_send()
            for copy in halo_waits[side]:
                copy.wait_recv()

        keep = mask_ref[0:1, side : side + 1].astype(jnp.float32) * near_scale
        tile = keep * kernel_tile(points_ref[...], halo_xyz[side])
        image_ref[...] = image_ref[...] + matmul_hi(tile, halo_res[side])

    for wave in range(levels + chunks - 1):
        for level in reversed(range(levels)):
            if 0 <= wave - level < chunks:
                step(level, wave - level)
        if wave == chunks - 1:
            near_side(0)
        if wave == chunks:
            near_side(1)


def local_image(
    coords, residual_in, link_mask, compress, expand, level_gain, level_couple, partner_perm
):
    n_row, n_col = lax.axis_size("row"), lax.axis_size("col")
    points, width = residual_in.shape
    rank = compress.shape[1]
    chunks = width // LANES
    levels = ROW_LEVELS + COL_LEVELS
    vmem = pl.BlockSpec(memory_space=pltpu.VMEM)
    dma = pltpu.SemaphoreType.DMA
    f32 = jnp.float32
    return pl.pallas_call(
        functools.partial(image_kernel, n_row, n_col),
        out_shape=jax.ShapeDtypeStruct((points, width), f32),
        in_specs=[vmem] * 9,
        out_specs=vmem,
        scratch_shapes=[
            pltpu.VMEM((levels, rank, rank), f32),
            pltpu.VMEM((levels, rank, LANES), f32),
            pltpu.VMEM((levels - 1, chunks, rank, LANES), f32),
            pltpu.VMEM((levels - 1, chunks, rank, LANES), f32),
            pltpu.VMEM((chunks, points, LANES), f32),
            pltpu.VMEM((points, rank), f32),
            pltpu.VMEM((2, points, width), f32),
            pltpu.VMEM((2, coords.shape[0], points), f32),
            dma((2,)),
            dma((chunks, 2)),
            dma((2, 2)),
            dma((2, 2)),
            dma((levels - 1, chunks, 2)),
        ],
        compiler_params=pltpu.CompilerParams(collective_id=2, has_side_effects=True),
        name="image_all",
    )(
        coords, coords.T, residual_in, link_mask, compress, expand, level_gain, level_couple,
        partner_perm,
    )


def shards(
    coords, residual_in, link_mask, compress, expand, level_gain, level_couple, partner_perm
):
    image = local_image(
        coords, residual_in, link_mask, compress, expand, level_gain, level_couple, partner_perm
    )
    return finish_step(image, residual_in)


def solution(mesh):
    return jax.shard_map(
        shards,
        mesh=mesh,
        in_specs=(
            P(None, ("row", "col")),
            P(("row", "col"), None),
            P(("row", "col"), None),
            P(("row", "col"), None),
            P(("row", "col"), None),
            P(("row", "col"), None),
            P(("row", "col"), None),
            P(("row", "col"), None, None),
        ),
        out_specs=(P(("row", "col"), None), P()),
        check_vma=False,
    )
```

```python
import functools

import jax
import jax.numpy as jnp
from jax import lax
from jax.experimental import pallas as pl
from jax.experimental.pallas import tpu as pltpu
from jax.sharding import PartitionSpec as P

ROW_LEVELS = 2
COL_LEVELS = 3


WAVENUM = 6.0
SOFTEN = 0.01
LANES = 128
SUB = 8
GRAM_STREAMS = 3
CROSS_STREAMS = 2
MESH = pl.DeviceIdType.MESH


def kernel_tile(own_cols, other_rows):
    dist_sq = (own_cols[:, 0:1] - other_rows[0:1, :]) ** 2
    dist_sq = dist_sq + (own_cols[:, 1:2] - other_rows[1:2, :]) ** 2
    dist_sq = dist_sq + (own_cols[:, 2:3] - other_rows[2:3, :]) ** 2
    return jnp.cos(WAVENUM * jnp.sqrt(dist_sq)) / jnp.sqrt(dist_sq + SOFTEN)


def matmul_hi(left, right):
    return jnp.dot(
        left, right, precision=lax.Precision.HIGHEST, preferred_element_type=jnp.float32
    )


def inner_cols(left, right):
    return lax.dot_general(
        left,
        right,
        (((0,), (0,)), ((), ())),
        precision=lax.Precision.HIGHEST,
        preferred_element_type=jnp.float32,
    )


def padded(rows, devices, streams):
    unit = SUB * devices * streams
    return -(-rows // unit) * unit


def gram_slots(tiles):
    return [(i, j) for i in range(tiles) for j in range(i, tiles)]


def stream_orders(n_row, n_col, streams):
    col_bits = [("col", b) for b in range(n_col.bit_length() - 1)]
    row_bits = [("row", b) for b in range(n_row.bit_length() - 1)]
    core, side = col_bits[:1], col_bits[1:]
    lead = side + row_bits[:1]
    return [core + lead[s:] + lead[:s] + row_bits[1:] for s in range(streams)]


def bit_of(step):
    axis, b = step
    return lax.axis_index(axis) // (1 << b) % 2


def flipped(step):
    axis, b = step
    place = {"row": lax.axis_index("row"), "col": lax.axis_index("col")}
    place[axis] = place[axis] + (1 - 2 * bit_of(step)) * (1 << b)
    return (place["row"], place["col"])


def sum_phases(orders, buf, land, full, rs_send, rs_recv, ag_send, ag_recv):
    streams, steps = len(orders), len(orders[0])
    share = buf.shape[0] // streams
    starts = [s * share for s in range(streams)]
    history = []
    land_at = 0
    size = share
    for t in range(steps):
        half = size // 2
        copies = []
        keeps = []
        for s in range(streams):
            step = orders[s][t]
            bit = bit_of(step)
            keeps.append(pl.multiple_of(starts[s] + bit * half, SUB))
            give = pl.multiple_of(starts[s] + (1 - bit) * half, SUB)
            copy = pltpu.make_async_remote_copy(
                src_ref=buf.at[pl.ds(give, half), :],
                dst_ref=land.at[pl.ds(s * share + land_at, half), :],
                send_sem=rs_send.at[s, t],
                recv_sem=rs_recv.at[s, t],
                device_id=flipped(step),
                device_id_type=MESH,
            )
            copy.start()
            copies.append(copy)
        yield
        for s in range(streams):
            copies[s].wait()
            here = pl.ds(keeps[s], half)
            got = land[s * share + land_at : s * share + land_at + half, :]
            if t == steps - 1:
                full[here, :] = buf[here, :] + got
            else:
                buf[here, :] = buf[here, :] + got
        history.append(keeps)
        starts = keeps
        land_at += half
        size = half
    for t in reversed(range(steps)):
        copies = []
        for s in range(streams):
            here = full.at[pl.ds(history[t][s], size), :]
            copy = pltpu.make_async_remote_copy(
                src_ref=here,
                dst_ref=here,
                send_sem=ag_send.at[s, t],
                recv_sem=ag_recv.at[s, t],
                device_id=flipped(orders[s][t]),
                device_id_type=MESH,
            )
            copy.start()
            copies.append(copy)
        yield
        for copy in copies:
            copy.wait()
        size = size * 2


def invert_panels(tile, count):
    size = tile.shape[0]
    lane = lax.broadcasted_iota(jnp.int32, (SUB, size), 1)
    sub = lax.broadcasted_iota(jnp.int32, (SUB, size), 0)

    def panel(_, mat):
        top, rest = mat[:SUB], mat[SUB:]
        top_cols = [jnp.broadcast_to(top[:, m : m + 1], (SUB, size)) for m in range(SUB)]
        top = jnp.where(lane < SUB, 0.0, top)
        for i in range(SUB):
            pivot = jnp.broadcast_to(top_cols[i][i : i + 1], (SUB, size))
            inv = 1.0 / pivot
            own = sub == i
            factor = jnp.where(own, 0.0, top_cols[i])
            row = jnp.broadcast_to(top[i : i + 1], (SUB, size)) * inv
            row = jnp.where(lane == i, inv, row)
            top = jnp.where(own, row, top - factor * row)
            for m in range(i + 1, SUB):
                entry = jnp.broadcast_to(top_cols[m][i : i + 1], (SUB, size)) * inv
                top_cols[m] = jnp.where(own, entry, top_cols[m] - factor * entry)
        lane_rest = lax.broadcasted_iota(jnp.int32, rest.shape, 1)
        fresh = jnp.where(lane_rest < SUB, 0.0, rest)
        for m in range(SUB):
            fresh = fresh - jnp.broadcast_to(rest[:, m : m + 1], rest.shape) * top[m : m + 1]
        mat = jnp.concatenate([fresh, top], axis=0)
        return pltpu.roll(mat, size - SUB, 1)

    return lax.fori_loop(0, count, panel, tile)


def finish_kernel(
    n_row, n_col, image_ref, res_ref, new_ref, norm_ref,
    g_buf, g_land, g_full, c_buf, c_land, c_full, g_ref, c_ref, inv_ref, *sems
):
    width = image_ref.shape[1]
    tiles = width // LANES
    points_total = image_ref.shape[0] * n_row * n_col
    gram_rows = tiles * (tiles + 1) // 2 * LANES
    g_orders = stream_orders(n_row, n_col, GRAM_STREAMS)
    c_orders = stream_orders(n_row, n_col, CROSS_STREAMS)

    barrier = pltpu.get_barrier_semaphore()
    for step in g_orders[0]:
        pl.semaphore_signal(barrier, inc=1, device_id=flipped(step), device_id_type=MESH)

    slot = 0
    for i in range(tiles):
        rows = inner_cols(image_ref[:, i * LANES : (i + 1) * LANES], image_ref[:, i * LANES :])
        for j in range(tiles - i):
            at = slot * LANES
            g_buf[at : at + LANES, :] = rows[:, j * LANES : (j + 1) * LANES]
            slot += 1
    g_buf[gram_rows:, :] = jnp.zeros((g_buf.shape[0] - gram_rows, LANES), jnp.float32)
    squares = jnp.sum(res_ref[...] * res_ref[...], axis=0, keepdims=True)
    for j in range(tiles):
        g_buf[gram_rows + j : gram_rows + j + 1, :] = squares[:, j * LANES : (j + 1) * LANES]

    pl.semaphore_wait(barrier, len(g_orders[0]))
    gram_sum = sum_phases(g_orders, g_buf, g_land, g_full, *sems[:4])
    next(gram_sum)
    for i in range(tiles):
        rows = inner_cols(image_ref[:, i * LANES : (i + 1) * LANES], res_ref[...])
        for j in range(tiles):
            at = j * width + i * LANES
            c_buf[at : at + LANES, :] = rows[:, j * LANES : (j + 1) * LANES]
    spare = c_buf.shape[0] - tiles * width
    if spare:
        c_buf[tiles * width :, :] = jnp.zeros((spare, LANES), jnp.float32)
    for _ in gram_sum:
        pass
    cross_sum = sum_phases(c_orders, c_buf, c_land, c_full, *sems[4:])
    next(cross_sum)

    for slot, (i, j) in enumerate(gram_slots(tiles)):
        g_ref[i * LANES : (i + 1) * LANES, j * LANES : (j + 1) * LANES] = g_full[
            slot * LANES : (slot + 1) * LANES, :
        ]
    steps = len(c_orders[0])
    quota = [3, 3] + [1] * (steps - 3) + [2]
    quota = quota + quota[::-1]
    done = [0]

    def tick():
        done[0] += 1
        if quota and done[0] >= quota[0]:
            quota.pop(0)
            done[0] = 0
            next(cross_sum, None)

    pieces = 4
    panels = LANES // SUB // pieces
    for k in range(tiles):
        lo, hi = k * LANES, (k + 1) * LANES
        inverse = g_ref[lo:hi, lo:hi]
        for _ in range(pieces):
            inverse = invert_panels(inverse, panels)
            tick()
        inv_ref[lo:hi, :] = inverse
        if hi < width:
            link = g_ref[lo:hi, hi:]
            right = matmul_hi(inverse, link)
            for i in range(k + 1, tiles):
                a, b = i * LANES, (i + 1) * LANES
                g_ref[a:b, a:] = g_ref[a:b, a:] - inner_cols(
                    link[:, a - hi : b - hi], right[:, a - hi :]
                )
            g_ref[lo:hi, hi:] = right
            tick()
    for _ in cross_sum:
        pass

    for j in range(tiles):
        c_ref[:, j * LANES : (j + 1) * LANES] = c_full[j * width : (j + 1) * width, :]
    for k in range(tiles):
        lo, hi = k * LANES, (k + 1) * LANES
        part = c_ref[lo:hi, :]
        c_ref[lo:hi, :] = matmul_hi(inv_ref[lo:hi, :], part)
        if hi < width:
            c_ref[hi:, :] = c_ref[hi:, :] - inner_cols(g_ref[lo:hi, hi:], part)
    for k in reversed(range(tiles - 1)):
        lo, hi = k * LANES, (k + 1) * LANES
        c_ref[lo:hi, :] = c_ref[lo:hi, :] - matmul_hi(g_ref[lo:hi, hi:], c_ref[hi:, :])

    new_ref[...] = res_ref[...] - matmul_hi(image_ref[...], c_ref[...])
    for j in range(tiles):
        cols = slice(j * LANES, (j + 1) * LANES)
        cross = c_full[j * width : (j + 1) * width, :]
        explained = jnp.sum(c_ref[:, cols] * cross, axis=0, keepdims=True)
        left = g_full[gram_rows + j : gram_rows + j + 1, :] - explained
        norm_ref[:, cols] = jnp.sqrt(jnp.maximum(left, 0.0) / points_total)


def finish_step(image, residual_in):
    n_row, n_col = lax.axis_size("row"), lax.axis_size("col")
    width = residual_in.shape[1]
    tiles = width // LANES
    gram_total = padded(tiles * (tiles + 1) // 2 * LANES + SUB, n_row * n_col, GRAM_STREAMS)
    cross_total = padded(tiles * width, n_row * n_col, CROSS_STREAMS)
    steps = len(stream_orders(n_row, n_col, 1)[0])
    vmem = pl.BlockSpec(memory_space=pltpu.VMEM)
    new_residual, norms = pl.pallas_call(
        functools.partial(finish_kernel, n_row, n_col),
        out_shape=(
            jax.ShapeDtypeStruct(residual_in.shape, jnp.float32),
            jax.ShapeDtypeStruct((1, width), jnp.float32),
        ),
        in_specs=[vmem] * 2,
        out_specs=(vmem, vmem),
        scratch_shapes=[pltpu.VMEM((gram_total, LANES), jnp.float32)] * 3
        + [pltpu.VMEM((cross_total, LANES), jnp.float32)] * 3
        + [pltpu.VMEM((width, width), jnp.float32)] * 2
        + [pltpu.VMEM((width, LANES), jnp.float32)]
        + [pltpu.SemaphoreType.DMA((GRAM_STREAMS, steps))] * 4
        + [pltpu.SemaphoreType.DMA((CROSS_STREAMS, steps))] * 4,
        compiler_params=pltpu.CompilerParams(collective_id=1, has_side_effects=True),
        name="finish_all",
    )(image, residual_in)
    return new_residual, norms[0]


def image_kernel(
    n_row, n_col,
    coords_ref, points_ref, res_ref, mask_ref, comp_ref, exp_ref, gain_ref, couple_ref, perm_ref,
    image_ref,
    mixed, gains, coef, land, land_res, land_comp, halo_res, halo_xyz,
    comp_sems, res_sems, halo_sems, xyz_sems, level_sems,
):
    rank = comp_ref.shape[1]
    width = res_ref.shape[1]
    chunks = width // LANES
    levels = ROW_LEVELS + COL_LEVELS
    at_row, at_col = lax.axis_index("row"), lax.axis_index("col")
    group = at_row * n_col + at_col
    has_side = (group > 0, group < n_row * n_col - 1)

    def partner_of(level):
        if level < ROW_LEVELS:
            bit = n_row.bit_length() - 2 - level
            return (at_row + (1 - 2 * (at_row // (1 << bit) % 2)) * (1 << bit), at_col)
        bit = n_col.bit_length() - 2 - (level - ROW_LEVELS)
        return (at_row, at_col + (1 - 2 * (at_col // (1 << bit) % 2)) * (1 << bit))

    def beside(side):
        other = group + (2 * side - 1)
        return (other // n_col, other % n_col)

    def remote(src, dst, sems, where):
        return pltpu.make_async_remote_copy(
            src_ref=src,
            dst_ref=dst,
            send_sem=sems.at[0],
            recv_sem=sems.at[1],
            device_id=where,
            device_id_type=MESH,
        )

    barrier = pltpu.get_barrier_semaphore()
    for level in range(levels):
        pl.semaphore_signal(barrier, inc=1, device_id=partner_of(level), device_id_type=MESH)
    for side in range(2):
        @pl.when(has_side[side])
        def _():
            pl.semaphore_signal(barrier, inc=1, device_id=beside(side), device_id_type=MESH)
    sides = jnp.minimum(group, 1) + jnp.minimum(n_row * n_col - 1 - group, 1)
    pl.semaphore_wait(barrier, levels + sides)

    def cols(k):
        return pl.ds(k * LANES, LANES)

    comp_copy = remote(comp_ref, land_comp, comp_sems, partner_of(0))
    comp_copy.start()
    res_copies = []
    for k in range(chunks):
        copy = remote(res_ref.at[:, cols(k)], land_res.at[k], res_sems.at[k], partner_of(0))
        copy.start()
        res_copies.append(copy)
    halo_copies = [
        (
            remote(coords_ref, halo_xyz.at[1 - side], xyz_sems.at[side], beside(side)),
            remote(res_ref, halo_res.at[1 - side], halo_sems.at[side], beside(side)),
        )
        for side in range(2)
    ]
    halo_waits = [
        (
            remote(coords_ref, halo_xyz.at[side], xyz_sems.at[1 - side], beside(side)),
            remote(res_ref, halo_res.at[side], halo_sems.at[1 - side], beside(side)),
        )
        for side in range(2)
    ]
    for side in range(2):
        @pl.when(has_side[side])
        def _():
            halo_copies[side][0].start()
            halo_copies[side][1].start()

        @pl.when(jnp.logical_not(has_side[side]))
        def _():
            halo_xyz[side] = jnp.zeros(halo_xyz.shape[1:], jnp.float32)
            halo_res[side] = jnp.zeros(halo_res.shape[1:], jnp.float32)

    down = lax.broadcasted_iota(jnp.int32, (rank, rank), 0)
    across = lax.broadcasted_iota(jnp.int32, (rank, rank), 1)
    for level in range(levels):
        here = slice(level * rank, (level + 1) * rank)
        taken = jnp.where(down == perm_ref[0, level : level + 1, :], 1.0, 0.0)
        mixed[level] = lax.dot_general(
            couple_ref[:, here],
            taken,
            (((1,), (1,)), ((), ())),
            precision=lax.Precision.HIGHEST,
            preferred_element_type=jnp.float32,
        )
        spread = jnp.where(down == across, gain_ref[:, here], 0.0)
        gains[level] = jnp.broadcast_to(jnp.sum(spread, axis=1, keepdims=True), (rank, LANES))

    own = inner_cols(comp_ref[...], res_ref[...])
    near_scale = (3.0 * res_ref.shape[0]) ** (-0.5)
    own_tile = near_scale * kernel_tile(points_ref[...], coords_ref[...])
    image_ref[...] = 2.0 * res_ref[...] + matmul_hi(own_tile, res_ref[...])

    comp_copy.wait()
    first = lax.dot_general(
        mixed[0],
        land_comp[...],
        (((1,), (1,)), ((), ())),
        precision=lax.Precision.HIGHEST,
        preferred_element_type=jnp.float32,
    )

    copies = {}

    def step(level, k):
        if level == 0:
            res_copies[k].wait()
            fresh = gains[0] * own[:, k * LANES : (k + 1) * LANES] + matmul_hi(first, land_res[k])
        else:
            copies[level, k].wait()
            fresh = gains[level] * coef[level - 1, k] + matmul_hi(mixed[level], land[level - 1, k])
        if level == levels - 1:
            image_ref[:, cols(k)] = image_ref[:, cols(k)] + matmul_hi(exp_ref[...], fresh)
            return
        coef[level, k] = fresh
        copy = remote(coef.at[level, k], land.at[level, k], level_sems.at[level, k], partner_of(level + 1))
        copy.start()
        copies[level + 1, k] = copy

    def near_side(side):
        @pl.when(has_side[side])
        def _():
            for copy in halo_copies[side]:
                copy.wait_send()
            for copy in halo_waits[side]:
                copy.wait_recv()

        keep = mask_ref[0:1, side : side + 1].astype(jnp.float32) * near_scale
        tile = keep * kernel_tile(points_ref[...], halo_xyz[side])
        image_ref[...] = image_ref[...] + matmul_hi(tile, halo_res[side])

    for wave in range(levels + chunks - 1):
        for level in reversed(range(levels)):
            if 0 <= wave - level < chunks:
                step(level, wave - level)
        if wave == chunks - 1:
            near_side(0)
        if wave == chunks:
            near_side(1)


def local_image(
    coords, residual_in, link_mask, compress, expand, level_gain, level_couple, partner_perm
):
    n_row, n_col = lax.axis_size("row"), lax.axis_size("col")
    points, width = residual_in.shape
    rank = compress.shape[1]
    chunks = width // LANES
    levels = ROW_LEVELS + COL_LEVELS
    vmem = pl.BlockSpec(memory_space=pltpu.VMEM)
    dma = pltpu.SemaphoreType.DMA
    f32 = jnp.float32
    return pl.pallas_call(
        functools.partial(image_kernel, n_row, n_col),
        out_shape=jax.ShapeDtypeStruct((points, width), f32),
        in_specs=[vmem] * 9,
        out_specs=vmem,
        scratch_shapes=[
            pltpu.VMEM((levels, rank, rank), f32),
            pltpu.VMEM((levels, rank, LANES), f32),
            pltpu.VMEM((levels - 1, chunks, rank, LANES), f32),
            pltpu.VMEM((levels - 1, chunks, rank, LANES), f32),
            pltpu.VMEM((chunks, points, LANES), f32),
            pltpu.VMEM((points, rank), f32),
            pltpu.VMEM((2, points, width), f32),
            pltpu.VMEM((2, coords.shape[0], points), f32),
            dma((2,)),
            dma((chunks, 2)),
            dma((2, 2)),
            dma((2, 2)),
            dma((levels - 1, chunks, 2)),
        ],
        compiler_params=pltpu.CompilerParams(collective_id=2, has_side_effects=True),
        name="image_all",
    )(
        coords, coords.T, residual_in, link_mask, compress, expand, level_gain, level_couple,
        partner_perm,
    )


def shards(
    coords, residual_in, link_mask, compress, expand, level_gain, level_couple, partner_perm
):
    image = local_image(
        coords, residual_in, link_mask, compress, expand, level_gain, level_couple, partner_perm
    )
    return finish_step(image, residual_in)


def solution(mesh):
    return jax.shard_map(
        shards,
        mesh=mesh,
        in_specs=(
            P(None, ("row", "col")),
            P(("row", "col"), None),
            P(("row", "col"), None),
            P(("row", "col"), None),
            P(("row", "col"), None),
            P(("row", "col"), None),
            P(("row", "col"), None),
            P(("row", "col"), None, None),
        ),
        out_specs=(P(("row", "col"), None), P()),
        check_vma=False,
    )
```
